32 devices in a mesh: slab: 8 (over y, x, core), energy: 4 (over z).
Axes of the slice: x: 2, y: 2, z: 4, core: 2. Of those that a mesh axis runs over, the one named last changes fastest.
Arguments:
- onsite: float32 [8, 256, 256], P('slab'), may hold values from -1.4 to 0.3, as said below
- coupling: float32 [8, 256, 256], P('slab'), may hold values from -0.25 to 1.6
- pattern: int32 [8, 4, 4], P('slab'), may hold values 0 or 1
- contact_rates: float32 [2, 256], replicated, may hold values from 1 to 3
- energy_index: int32 [16], P('energy'), parts along dimension 0, may hold values from 0 to 31
Outputs:
- spectral: float32 [8, 16, 256], P('slab', 'energy'), parts along dimension 1
- transmission: float32 [16], P('energy'), parts along dimension 0
The draws below stay inside these ranges and needn't reach their ends.
There are 4 independent parts, one for each index of `energy`. The reference program is written for one: setup_inputs(seed, part) draws one part's arguments, and reference() takes and returns one part's arrays. A program takes and returns all parts, laid end to end along the dimension named above; an argument that names none is the same for every part. Nothing has to cross between parts.
Inputs may be any that keep to these rules, and one draw needn't show every extreme that they name: Every onsite block is symmetric.
All inputs are finite; a program needn't handle non-finite values. No bound on the sum of `pattern` on one device may be relied on, other than what follows from the above.
Results may differ from the reference program's by a relative error of at most 0.00012.
Values sent between devices are 32-bit elements; how exact they have to be, the bound alone decides.
A program may use at most 64 MiB of HBM per device.

```python
import math
import jax
import jax.numpy as jnp
from jax import lax

W = 256
NT = 4
NE = 4
ITERS = 2
GRID = 32
NS = 8
MID = 4


def draw_onsite(key, part):
    key_offdiag, key_levels = jax.random.split(key)
    entries = jnp.clip(jax.random.normal(key_offdiag, (NS, W, W), jnp.float32), -6.0, 6.0) * (0.17 / math.sqrt(W))
    symmetric = (entries + jnp.swapaxes(entries, 1, 2)) * 0.70710678
    levels = jax.random.uniform(key_levels, (NS, W), jnp.float32, -1.4, -0.8)
    diagonal_mask = jnp.eye(W, dtype=bool)
    return jnp.where(diagonal_mask[None, :, :], levels[:, None, :], symmetric)


def draw_coupling(key, part):
    key_strength, key_rest = jax.random.split(jax.random.fold_in(key, 17))
    strengths = jax.random.uniform(key_strength, (NS, W), jnp.float32, 1.3, 1.6)
    rest = jnp.clip(jax.random.normal(key_rest, (NS, W, W), jnp.float32), -6.0, 6.0) * (0.11 / math.sqrt(W))
    diagonal_mask = jnp.eye(W, dtype=bool)
    return jnp.where(diagonal_mask[None, :, :], strengths[:, None, :], rest)


def set_ends(array, rng, least, top_value):
    index_at = [jax.random.randint(jax.random.fold_in(rng, axis), (), 0, length) for axis, length in enumerate(array.shape)]
    main_axis = array.shape.index(max(array.shape))
    neighbour = index_at[:main_axis] + [(index_at[main_axis] + 1) % array.shape[main_axis]] + index_at[main_axis + 1:]
    return array.at[tuple(index_at)].set(least).at[tuple(neighbour)].set(top_value)


def setup_inputs(seed: int = 0, part: int = 0) -> dict:
    arg_keys = jax.random.split(jax.random.key(seed), 6)
    own_keys = jax.random.split(jax.random.fold_in(arg_keys[5], part), 6)
    onsite = draw_onsite(jax.random.fold_in(arg_keys[5], 71), part)
    coupling = draw_coupling(jax.random.fold_in(arg_keys[5], 71), part)
    pattern = set_ends((jax.random.randint(arg_keys[2], (NS, NT, NT), 0, 8) < 7).astype(jnp.int32), jax.random.fold_in(arg_keys[2], 1), 0, 1)
    contact_rates = jnp.clip(jnp.exp(jax.random.uniform(arg_keys[3], (2, W), jnp.float32, math.log(1.0), math.log(3.0))), 1.0, 3.0)
    energy_index = set_ends(jax.random.randint(own_keys[4], (NE,), 0, GRID), jax.random.fold_in(own_keys[4], 1), 0, GRID - 1).astype(jnp.int32)
    return dict(onsite=onsite, coupling=coupling, pattern=pattern, contact_rates=contact_rates, energy_index=energy_index)


energy_floor = -0.2
energy_spacing = 0.0125
broadening = 0.3
highest = lax.Precision.HIGHEST


def product(left_factor, right_factor):
    return jnp.dot(left_factor, right_factor, preferred_element_type=jnp.float32, precision=highest)


def complex_product(left_factor, right_factor):
    real_real = product(left_factor[0], right_factor[0])
    imag_imag = product(left_factor[1], right_factor[1])
    summed = product(left_factor[0] + left_factor[1], right_factor[0] + right_factor[1])
    return jnp.stack([real_real - imag_imag, summed - real_real - imag_imag])


def schur_after(coupling_block, greens):
    halfway = jnp.stack([product(greens[0], coupling_block), product(greens[1], coupling_block)])
    transposed = coupling_block.T
    return jnp.stack([product(transposed, halfway[0]), product(transposed, halfway[1])])


def schur_before(coupling_block, greens):
    transposed = coupling_block.T
    halfway = jnp.stack([product(greens[0], transposed), product(greens[1], transposed)])
    return jnp.stack([product(coupling_block, halfway[0]), product(coupling_block, halfway[1])])


def invert(matrix):
    orbitals = matrix.shape[1]
    diag_real = jnp.diagonal(matrix[0])
    diag_imag = jnp.diagonal(matrix[1])
    modulus = diag_real * diag_real + diag_imag * diag_imag
    start_real = diag_real / modulus
    start_imag = -diag_imag / modulus
    identity = jnp.eye(orbitals, dtype=jnp.float32)
    applied_real = matrix[0] * start_real[None, :] - matrix[1] * start_imag[None, :]
    applied_imag = matrix[0] * start_imag[None, :] + matrix[1] * start_real[None, :]
    scaled_real = start_real[:, None] * applied_real - start_imag[:, None] * applied_imag
    scaled_imag = start_real[:, None] * applied_imag + start_imag[:, None] * applied_real
    approx = jnp.stack([2.0 * identity * start_real[None, :] - scaled_real,
                        2.0 * identity * start_imag[None, :] - scaled_imag])
    for iteration in range(ITERS - 1):
        applied = complex_product(matrix, approx)
        approx = 2.0 * approx - complex_product(approx, applied)
    return approx


def green_block(energy, onsite_block, self_energy):
    identity = jnp.eye(onsite_block.shape[0], dtype=jnp.float32)
    real_part = energy * identity - onsite_block - self_energy[0]
    imag_part = broadening * identity - self_energy[1]
    return invert(jnp.stack([real_part, imag_part]))


def spectral_row(greens):
    return -2.0 * jnp.diagonal(greens[1])


def transmitted(left_energy, right_energy, greens):
    gamma_left = -2.0 * left_energy[1]
    gamma_right = -2.0 * right_energy[1]
    forward_real = product(gamma_left, greens[0])
    forward_imag = product(gamma_left, greens[1])
    backward_real = product(gamma_right, greens[0].T)
    backward_imag = -product(gamma_right, greens[1].T)
    return jnp.sum(forward_real * backward_real.T) - jnp.sum(forward_imag * backward_imag.T)


def contact_energy(rates):
    identity = jnp.eye(rates.shape[0], dtype=jnp.float32)
    return jnp.stack([jnp.zeros_like(identity), identity * (-0.5 * rates)[None, :]])


def mask_coupling(coupling, pattern):
    slab_count = coupling.shape[0]
    orbitals = coupling.shape[1]
    tile_count = pattern.shape[1]
    tile_size = orbitals // tile_count
    blocks = coupling.reshape(slab_count, tile_count, tile_size, tile_count, tile_size)
    blocks = blocks * pattern.astype(jnp.float32)[:, :, None, :, None]
    return blocks.reshape(slab_count, orbitals, orbitals)


def reference(onsite, coupling, pattern, contact_rates, energy_index):
    masked = mask_coupling(coupling, pattern)
    energies = energy_floor + energy_spacing * energy_index.astype(jnp.float32)
    left_contact = contact_energy(contact_rates[0])
    right_contact = contact_energy(contact_rates[1])

    def one_energy(energy):
        def left_step(carried, pieces):
            greens = green_block(energy, pieces[0], carried)
            return schur_after(pieces[1], greens), carried

        def right_step(carried, pieces):
            greens = green_block(energy, pieces[0], carried)
            return schur_before(pieces[1], greens), carried

        unused, lefts = lax.scan(left_step, left_contact, (onsite[:NS - 1], masked[:NS - 1]))
        last_left = schur_after(masked[NS - 2], green_block(energy, onsite[NS - 2], lefts[NS - 2]))
        lefts = jnp.concatenate([lefts, last_left[None]], axis=0)
        lowest, uppers = lax.scan(right_step, right_contact, (onsite[1:][::-1], masked[:NS - 1][::-1]))
        rights = jnp.concatenate([lowest[None], uppers[::-1]], axis=0)

        def slab_spectrum(pieces):
            return spectral_row(green_block(energy, pieces[0], pieces[1] + pieces[2]))

        spectra = lax.map(slab_spectrum, (onsite, lefts, rights))
        middle = green_block(energy, onsite[MID], lefts[MID] + rights[MID])
        return spectra, transmitted(lefts[MID], rights[MID], middle)

    spectra, crossing = lax.map(one_energy, energies)
    return jnp.transpose(spectra, (1, 0, 2)), crossing
```

```python
import functools

import jax
import jax.numpy as jnp
from jax import lax
from jax.experimental import pallas as pl
from jax.experimental.pallas import tpu as pltpu
from jax.sharding import PartitionSpec as P

energy_floor = -0.2
energy_spacing = 0.0125
broadening = 0.3
MESH = pl.DeviceIdType.MESH
f32, bf16 = jnp.float32, jnp.bfloat16


def split(x):
    high = x.astype(bf16)
    return high, (x - high.astype(f32)).astype(bf16)


def product(left, right):
    return jnp.dot(
        jnp.concatenate([left[0], left[0], left[1]], axis=1),
        jnp.concatenate([right[0], right[1], right[0]], axis=0),
        preferred_element_type=f32,
    )


def complex_product(left, right):
    first = product(left[0], right[0])
    second = product(left[1], right[1])
    third = product(left[2], right[2])
    return first - second, third - first - second


def split3(real, imag):
    return split(real), split(imag), split(real + imag)


def exclusive(index, other, count):
    if count & (count - 1):
        return (index + other) % count
    total, bit = 0, 1
    while bit < count:
        total = total + (((index // bit) + (other // bit) % 2) % 2) * bit
        bit *= 2
    return total


def kernel(
    n, ne, w,
    onsite_in, coupling_in, pattern_ref, rates_ref, index_ref,
    spectral_ref, crossing_ref,
    raw, o_buf, m_buf, bare, hist, other, current, factor, rows, crossing_own, rows_in, crossing_in,
    local_sem, o_send, m_send, o_relay, m_relay, f_send, o_recv, m_recv,
    s_send, s_recv, r_send, r_recv, t_send, t_recv,
):
    half = n // 2
    group = 2 * ne
    me = lax.axis_index("slab")
    side = me % 2
    partner = me + 1 - 2 * side
    chip = me // 2
    mine = chip % ne
    base = (me // group) * group
    square = half == 4

    def slab_at(t):
        return t + side * (n - 1 - 2 * t)

    def coupling_at(t):
        return t + side * (n - 2 - 2 * t)

    def remote(src, dst, send, recv, target):
        return pltpu.make_async_remote_copy(
            src_ref=src, dst_ref=dst, send_sem=send, recv_sem=recv,
            device_id={"slab": target}, device_id_type=MESH,
        )

    own_o = pltpu.make_async_copy(onsite_in.at[0], raw.at[0], local_sem.at[0])
    own_m = pltpu.make_async_copy(coupling_in.at[0], raw.at[1], local_sem.at[1])
    own_o.start()
    own_m.start()

    barrier = pltpu.get_barrier_semaphore()
    for step in range(1, n):
        pl.semaphore_signal(
            barrier, inc=1, device_id={"slab": (me + step) % n}, device_id_type=MESH
        )

    h = w // 2
    tile_row = lax.broadcasted_iota(jnp.int32, (h, h), 0)
    tile_column = lax.broadcasted_iota(jnp.int32, (h, h), 1)

    def packed(block):
        last = block[h:, h:]
        o_buf[me, :h, :h] = jnp.where(tile_row >= tile_column, block[:h, :h], last)
        o_buf[me, :h, h:] = block[:h, h:]
        diag = jnp.sum(jnp.where(tile_row == tile_column, last, 0.0), axis=0, keepdims=True)
        o_buf[me, h:, :] = jnp.broadcast_to(jnp.concatenate([diag, diag], axis=1), (8, w))

    def unpacked(j):
        both = o_buf[j, :h, :h]
        corner = o_buf[j, :h, h:]
        turned = both.T
        first = jnp.where(tile_row >= tile_column, both, turned)
        last = jnp.where(tile_row < tile_column, both, turned)
        last = jnp.where(tile_row == tile_column, o_buf[j, h : h + 1, :h], last)
        return jnp.concatenate(
            [
                jnp.concatenate([first, corner], axis=1),
                jnp.concatenate([corner.T, last], axis=1),
            ],
            axis=0,
        )

    own_o.wait()
    own_m.wait()
    packed(raw[0])
    tiles = pattern_ref.shape[1]
    size = w // tiles
    lane_tile = lax.broadcasted_iota(jnp.int32, (1, w), 1) // size
    for p in range(tiles):
        kept = jnp.zeros((1, w), f32)
        for q in range(tiles):
            kept = jnp.where(lane_tile == q, pattern_ref[0, p, q].astype(f32), kept)
        m_buf[me, p * size : (p + 1) * size, :] = raw[1, p * size : (p + 1) * size, :] * kept
    pl.semaphore_wait(barrier, n - 1)

    o_rows = o_buf.shape[1]
    o_cut = (o_rows // 16 + 1) * 8
    o_part = (pl.ds(0, o_cut), pl.ds(o_cut, o_rows - o_cut))
    m_part = (pl.ds(0, h), pl.ds(h, w - h))
    user = jnp.where(me < half, 0, 1)
    o_step = jnp.where(me < half, me, n - 1 - me)
    m_step = jnp.where(me < half, me, n - 2 - me)
    spread = (1, 2) if square else tuple(range(1, half))

    def stage(step):
        if not square:
            return jnp.zeros_like(step)
        return jnp.where(step < 2, step, step - 1)

    def o_copy(j, p, send, target):
        view = o_buf.at[j, o_part[p]]
        return remote(view, view, send, o_recv.at[j, p], target)

    def m_copy(j, p, send, target):
        view = m_buf.at[j, m_part[p]]
        return remote(view, view, send, m_recv.at[j, p], target)

    def own_copies(copy, send, act):
        for order in (0, 1):
            for k in spread:
                p = order if k == 1 else 1 - order
                act(copy(me, p, send.at[k, p], exclusive(chip, k, half) * 2 + user))

    def partner_copies(copy, send, act):
        @pl.when(side != user)
        def _():
            for p in (0, 1):
                act(copy(me, p, send.at[0, p], partner))

    def start(c):
        c.start()

    def finish(c):
        c.wait_send()

    def own_stage(s):
        pl.when(stage(o_step) == s)(lambda: own_copies(o_copy, o_send, start))
        pl.when((stage(m_step) == s) & (me < n - 1))(lambda: own_copies(m_copy, m_send, start))

    own_stage(0)
    partner_copies(o_copy, o_send, start)
    pl.when(me < n - 1)(lambda: partner_copies(m_copy, m_send, start))

    def passes(j, p):
        return chip == exclusive(j // 2, p + 1, half)

    def o_relayed(t, p):
        j = slab_at(t)
        return o_copy(j, p, o_relay.at[t], exclusive(chip, 2 - p, half) * 2 + side)

    def m_relayed(t, p):
        j = coupling_at(t)
        return m_copy(j, p, m_relay.at[t], exclusive(chip, 2 - p, half) * 2 + side)

    def m_shared(t):
        return (side == 1) & (t == half - 1)

    def relay_o(t):
        if square:
            for p in (0, 1):

                @pl.when(passes(slab_at(t), p))
                def _():
                    o_copy(slab_at(t), p, o_relay.at[t], partner).wait_recv()
                    o_relayed(t, p).start()

    def rest_o(t):
        j = slab_at(t)
        for p in (0, 1):
            waits = j != me
            if square:
                waits = waits & jnp.logical_not(passes(j, p))
            pl.when(waits)(lambda p=p: o_copy(j, p, o_relay.at[t], partner).wait_recv())

    def relay_m(t):
        if square:
            for p in (0, 1):

                @pl.when(passes(coupling_at(t), p) & jnp.logical_not(m_shared(t)))
                def _():
                    m_copy(coupling_at(t), p, m_relay.at[t], partner).wait_recv()
                    m_relayed(t, p).start()

    def handed(p):
        return m_copy(half - 1, p, f_send.at[p], partner)

    hands = (side == 0) & (partner != half - 1)

    def rest_m(t):
        j = coupling_at(t)
        for p in (0, 1):
            waits = j != me
            if square:
                waits = waits & (jnp.logical_not(passes(j, p)) | m_shared(t))
            pl.when(waits)(lambda p=p: m_copy(j, p, m_relay.at[t], partner).wait_recv())

        @pl.when(hands & (t == half - 1))
        def _():
            for p in (0, 1):
                handed(p).start()

    row_at = lax.broadcasted_iota(jnp.int32, (w, w), 0)
    column_at = lax.broadcasted_iota(jnp.int32, (w, w), 1)
    eye = row_at == column_at
    energy = energy_floor + energy_spacing * index_ref[mine].astype(f32)

    def scaled(real, imag):
        diag_real = jnp.sum(jnp.where(eye, real, 0.0), axis=0, keepdims=True)
        diag_imag = jnp.sum(jnp.where(eye, imag, 0.0), axis=0, keepdims=True)
        modulus = diag_real * diag_real + diag_imag * diag_imag
        xr = diag_real / modulus
        xi = -diag_imag / modulus
        xrc = jnp.sum(jnp.where(eye, xr, 0.0), axis=1, keepdims=True)
        xic = jnp.sum(jnp.where(eye, xi, 0.0), axis=1, keepdims=True)
        off_real = jnp.where(eye, 0.0, real)
        off_imag = jnp.where(eye, 0.0, imag)
        fr = off_real * xr - off_imag * xi
        fi = off_real * xi + off_imag * xr
        return (xr, xi, xrc, xic), (off_real, off_imag), (fr, fi)

    def completed(x, f, f_parts, f2):
        third = complex_product(f_parts, split3(*f2))
        hr = jnp.where(eye, 1.0, 0.0) - f[0] + f2[0] - third[0]
        hi = f2[1] - f[1] - third[1]
        xrc, xic = x[2], x[3]
        return xrc * hr - xic * hi, xrc * hi + xic * hr

    def diagonal(x, off, f, f2):
        xr, xi, xrc, xic = x
        zr = off[0] * xrc - off[1] * xic
        zi = off[0] * xic + off[1] * xrc
        wr = f[0] - f2[0]
        wi = f[1] - f2[1]
        dr = 1.0 + jnp.sum(zr * wr - zi * wi, axis=0, keepdims=True)
        di = jnp.sum(zr * wi + zi * wr, axis=0, keepdims=True)
        return -2.0 * (xr * di + xi * dr)

    def keep_factor(t):
        m = m_buf[coupling_at(t)]
        high, low = split(m)
        factor[t, side, 0] = high
        factor[t, side, 1] = low
        high, low = split(m.T)
        factor[t, 1 - side, 0] = high
        factor[t, 1 - side, 1] = low

    def inverted(a):
        x, off, f = scaled(*a)
        parts = split3(*f)
        f2 = complex_product(parts, parts)
        return completed(x, f, parts, f2)

    def stepped(g, first, second, out):
        gs = split(jnp.concatenate(g, axis=0))
        u = product(gs, (first[0], first[1]))
        us = split(jnp.concatenate([u[:w], u[w:]], axis=1))
        s = product((second[0], second[1]), us)
        out[0] = s[:, :w]
        out[1] = s[:, w:]

    def final(k, real, imag):
        x, off, f = scaled(real, imag)
        parts = split3(*f)
        f2 = complex_product(parts, parts)
        rows[k] = jnp.broadcast_to(diagonal(x, off, f, f2), (8, w))
        return x, f, parts, f2

    rates = jnp.where(side == 0, rates_ref[0:1, :], rates_ref[1:2, :])
    hist[0, 0] = jnp.zeros((w, w), f32)
    hist[0, 1] = jnp.where(eye, -0.5 * rates, 0.0)
    widths = jnp.where(eye, broadening, 0.0)

    relay_o(0)

    def outward(t, carry):
        rest_o(t)
        relay_m(t)
        own_stage(t + 1)
        level = jnp.where(eye, energy, 0.0) - unpacked(slab_at(t))
        bare[t] = level
        g = inverted((level - hist[t, 0], widths - hist[t, 1]))
        rest_m(t)
        pl.when(t < half - 1)(lambda: relay_o(jnp.minimum(t + 1, half - 1)))
        keep_factor(t)
        stepped(g, factor.at[t, 0], factor.at[t, 1], hist.at[t + 1])
        return carry

    lax.fori_loop(0, half, outward, 0)

    swap = remote(hist.at[half], other, s_send.at[0], s_recv.at[0], partner)
    swap.start()

    def row_copy(k):
        return remote(
            rows.at[k], rows_in.at[mine], r_send.at[k], r_recv.at[mine], slab_at(half - 1 - k)
        )

    def deliver(k):
        target = slab_at(half - 1 - k)

        @pl.when((target // group) == (me // group))
        def _():
            @pl.when(target == me)
            def _():
                rows_in[mine] = rows[k]

            @pl.when(target != me)
            def _():
                row_copy(k).start()

    def t_copy(k):
        return remote(
            crossing_own, crossing_in.at[mine], t_send.at[k - 1], t_recv.at[mine],
            base + (me - base + k) % group,
        )

    def behind(t, g):
        stepped(g, factor.at[t, 1], factor.at[t, 0], current)

    last = half - 1
    swap.wait_recv()
    real = bare[last] - other[0]
    imag = widths - other[1]
    x, f, parts, f2 = final(0, real - hist[last, 0], imag - hist[last, 1])

    @pl.when(side == 1)
    def _():
        gr, gi = completed(x, f, parts, f2)
        gamma_left = -2.0 * other[1]
        gamma_right = -2.0 * hist[last, 1]
        forward = product(split(gamma_left), split(jnp.concatenate([gr, gi], axis=1)))
        backward = product(split(jnp.concatenate([gr, gi], axis=0)), split(gamma_right))
        total = jnp.sum(forward[:, :w] * backward[:w] + forward[:, w:] * backward[w:])
        crossing_own[...] = jnp.full((8, 128), total, f32)

    behind(last - 1, inverted((real, imag)))

    def inward(k, carry):
        deliver(k - 1)
        t = last - k
        real = bare[t] - current[0]
        imag = widths - current[1]
        final(k, real - hist[t, 0], imag - hist[t, 1])
        behind(t - 1, inverted((real, imag)))
        return carry

    lax.fori_loop(1, last, inward, 0)

    @pl.when(side == 1)
    def _():
        crossing_in[mine] = crossing_own[...]
        for k in range(1, group):
            t_copy(k).start()

    deliver(last - 1)
    final(last, bare[0] - current[0] - hist[0, 0], widths - current[1] - hist[0, 1])
    deliver(last)

    def row_wait(e):
        remote(rows.at[0], rows_in.at[e], r_send.at[0], r_recv.at[e], partner).wait_recv()

    for e in range(ne):
        pl.when(base + 2 * e + user != me)(functools.partial(row_wait, e))

    def t_wait(e):
        remote(crossing_own, crossing_in.at[e], t_send.at[0], t_recv.at[e], partner).wait_recv()

    for e in range(ne):
        pl.when(base + 2 * e + 1 != me)(functools.partial(t_wait, e))
    for e in range(ne):
        spectral_ref[0, e : e + 1, :] = rows_in[e, 0:1, :]
        crossing_ref[e] = crossing_in[e, 0, 0]

    own_copies(o_copy, o_send, finish)
    partner_copies(o_copy, o_send, finish)

    @pl.when(me < n - 1)
    def _():
        own_copies(m_copy, m_send, finish)
        partner_copies(m_copy, m_send, finish)

    @pl.when(hands)
    def _():
        for p in (0, 1):
            handed(p).wait_send()

    swap.wait_send()

    @pl.when(side == 1)
    def _():
        for k in range(1, group):
            t_copy(k).wait_send()

    def drain(t, carry):
        if square:
            for p in (0, 1):
                pl.when(passes(slab_at(t), p))(lambda p=p: o_relayed(t, p).wait_send())
                pl.when(passes(coupling_at(t), p) & jnp.logical_not(m_shared(t)))(
                    lambda p=p: m_relayed(t, p).wait_send()
                )
        target = slab_at(half - 1 - t)

        @pl.when(((target // group) == (me // group)) & (target != me))
        def _():
            row_copy(t).wait_send()

        return carry

    lax.fori_loop(0, half, drain, 0)


def solution(mesh):
    n = mesh.shape["slab"]

    def on_device(onsite, coupling, pattern, contact_rates, energy_index):
        w = onsite.shape[1]
        ne = energy_index.shape[0]
        half = n // 2
        dma = pltpu.SemaphoreType.DMA
        return pl.pallas_call(
            functools.partial(kernel, n, ne, w),
            out_shape=(
                jax.ShapeDtypeStruct((1, ne, w), f32),
                jax.ShapeDtypeStruct((ne,), f32),
            ),
            in_specs=[
                pl.BlockSpec(memory_space=pl.ANY),
                pl.BlockSpec(memory_space=pl.ANY),
                pl.BlockSpec(memory_space=pltpu.SMEM),
                pl.BlockSpec(memory_space=pltpu.VMEM),
                pl.BlockSpec(memory_space=pltpu.SMEM),
            ],
            out_specs=(
                pl.BlockSpec(memory_space=pltpu.VMEM),
                pl.BlockSpec(memory_space=pltpu.SMEM),
            ),
            scratch_shapes=[
                pltpu.VMEM((2, w, w), f32),
                pltpu.VMEM((n, w // 2 + 8, w), f32),
                pltpu.VMEM((n, w, w), f32),
                pltpu.VMEM((half, w, w), f32),
                pltpu.VMEM((half + 1, 2, w, w), f32),
                pltpu.VMEM((2, w, w), f32),
                pltpu.VMEM((2, w, w), f32),
                pltpu.VMEM((half, 2, 2, w, w), bf16),
                pltpu.VMEM((half, 8, w), f32),
                pltpu.VMEM((8, 128), f32),
                pltpu.VMEM((ne, 8, w), f32),
                pltpu.VMEM((ne, 8, 128), f32),
                dma((2,)), dma((half, 2)), dma((half, 2)), dma((half,)), dma((half,)), dma((2,)), dma((n, 2)), dma((n, 2)),
                dma((1,)), dma((1,)), dma((half,)), dma((ne,)), dma((2 * ne - 1,)), dma((ne,)),
            ],
            compiler_params=pltpu.CompilerParams(
                collective_id=0, has_side_effects=True, vmem_limit_bytes=60 * 2**20
            ),
        )(onsite, coupling, pattern, contact_rates, energy_index)

    return jax.shard_map(
        on_device,
        mesh=mesh,
        in_specs=(
            P("slab", None, None),
            P("slab", None, None),
            P("slab", None, None),
            P(),
            P("energy"),
        ),
        out_specs=(P("slab", "energy", None), P("energy")),
        check_vma=False,
    )
```

```python
import functools

import jax
import jax.numpy as jnp
from jax import lax
from jax.experimental import pallas as pl
from jax.experimental.pallas import tpu as pltpu
from jax.sharding import PartitionSpec as P

energy_floor = -0.2
energy_spacing = 0.0125
broadening = 0.3
MESH = pl.DeviceIdType.MESH
f32, bf16 = jnp.float32, jnp.bfloat16


def split(x):
    high = x.astype(bf16)
    return high, (x - high.astype(f32)).astype(bf16)


def product(left, right):
    return jnp.dot(
        jnp.concatenate([left[0], left[0], left[1]], axis=1),
        jnp.concatenate([right[0], right[1], right[0]], axis=0),
        preferred_element_type=f32,
    )


def rounded(real, imag):
    return jnp.concatenate([real.astype(bf16), imag.astype(bf16)], axis=1)


def doubled(real, imag):
    real, imag = real.astype(bf16), imag.astype(bf16)
    return jnp.concatenate(
        [jnp.concatenate([real, imag], axis=1), jnp.concatenate([-imag, real], axis=1)], axis=0
    )


def complex_product(left, right):
    both = jnp.dot(left, doubled(*right), preferred_element_type=f32)
    width = both.shape[1] // 2
    return both[:, :width], both[:, width:]


def exclusive(index, other, count):
    if count & (count - 1):
        return (index + other) % count
    total, bit = 0, 1
    while bit < count:
        total = total + (((index // bit) + (other // bit) % 2) % 2) * bit
        bit *= 2
    return total


def kernel(
    n, ne, w,
    onsite_in, coupling_in, pattern_ref, rates_ref, index_ref,
    spectral_ref, crossing_ref,
    raw, o_buf, m_buf, hist, other, factor, rows, crossing_own, rows_in, crossing_in,
    local_sem, o_send, m_send, h_send, h_recv, o_fsend, m_fsend, o_recv, m_recv,
    s_send, s_recv, r_send, r_recv, t_send, t_recv,
):
    half = n // 2
    group = 2 * ne
    me = lax.axis_index("slab")
    side = me % 2
    partner = me + 1 - 2 * side
    mine = (me // 2) % ne
    base = (me // group) * group

    def slab_at(t):
        return t + side * (n - 1 - 2 * t)

    def coupling_at(t):
        return t + side * (n - 2 - 2 * t)

    def remote(src, dst, send, recv, target):
        return pltpu.make_async_remote_copy(
            src_ref=src, dst_ref=dst, send_sem=send, recv_sem=recv,
            device_id={"slab": target}, device_id_type=MESH,
        )

    own_o = pltpu.make_async_copy(onsite_in.at[0], raw.at[0], local_sem.at[0])
    own_m = pltpu.make_async_copy(coupling_in.at[0], raw.at[1], local_sem.at[1])
    own_o.start()
    own_m.start()

    barrier = pltpu.get_barrier_semaphore()
    for step in range(1, n):
        pl.semaphore_signal(
            barrier, inc=1, device_id={"slab": (me + step) % n}, device_id_type=MESH
        )

    h = w // 2
    tile_row = lax.broadcasted_iota(jnp.int32, (h, h), 0)
    tile_column = lax.broadcasted_iota(jnp.int32, (h, h), 1)

    def packed(block):
        last = block[h:, h:]
        o_buf[me, :h, :h] = jnp.where(tile_row >= tile_column, block[:h, :h], last)
        o_buf[me, :h, h:] = block[:h, h:]
        diag = jnp.sum(jnp.where(tile_row == tile_column, last, 0.0), axis=0, keepdims=True)
        o_buf[me, h:, :] = jnp.broadcast_to(jnp.concatenate([diag, diag], axis=1), (8, w))

    def unpacked(j):
        both = o_buf[j, :h, :h]
        corner = o_buf[j, :h, h:]
        turned = both.T
        first = jnp.where(tile_row >= tile_column, both, turned)
        last = jnp.where(tile_row < tile_column, both, turned)
        last = jnp.where(tile_row == tile_column, o_buf[j, h : h + 1, :h], last)
        return jnp.concatenate(
            [
                jnp.concatenate([first, corner], axis=1),
                jnp.concatenate([corner.T, last], axis=1),
            ],
            axis=0,
        )

    own_o.wait()
    own_m.wait()
    packed(raw[0])
    tiles = pattern_ref.shape[1]
    size = w // tiles
    lane_tile = lax.broadcasted_iota(jnp.int32, (1, w), 1) // size
    for p in range(tiles):
        kept = jnp.zeros((1, w), f32)
        for q in range(tiles):
            kept = jnp.where(lane_tile == q, pattern_ref[0, p, q].astype(f32), kept)
        m_buf[me, p * size : (p + 1) * size, :] = raw[1, p * size : (p + 1) * size, :] * kept
    pl.semaphore_wait(barrier, n - 1)

    square = half == 4
    chip = me // 2
    if square:
        aside = exclusive(chip, 1, half) * 2 + side
        above = exclusive(chip, 2, half) * 2 + side
        targets = [aside, above]
    else:
        aside = above = me
        targets = [exclusive(chip, k, half) * 2 + side for k in range(half - 1, 0, -1)]
    cut = w // 4
    top, bottom = pl.ds(0, cut), pl.ds(cut, w - cut)

    def o_part(j, k, target):
        return remote(o_buf.at[j], o_buf.at[j], o_send.at[k], o_recv.at[j], target)

    def top_part(j, k, target):
        return remote(
            m_buf.at[j, top], m_buf.at[j, top], h_send.at[k], h_recv.at[j], target
        )

    def bottom_part(j, k, target):
        return remote(
            m_buf.at[j, bottom], m_buf.at[j, bottom], m_send.at[k], m_recv.at[j], target
        )

    def used(j, act):
        pl.when(j < n - 1)(act)

    def send_first(j, k, target):
        o_part(j, k, target).start()
        used(j, lambda: top_part(j, k, target).start())

    def send_second(j, k, target):
        used(j, lambda: bottom_part(j, k, target).start())

    def arrived(buf, sems, j):
        remote(buf.at[j], buf.at[j], o_send.at[0], sems.at[j], partner).wait_recv()

    def direct(j):
        @pl.when((j != me) & (j != aside))
        def _():
            top_part(j, 0, partner).wait_recv()

        @pl.when((j != me) & (j != above))
        def _():
            bottom_part(j, 0, partner).wait_recv()

    if square:
        send_first(me, 0, aside)
        send_second(me, 1, above)
        outer = (chip == 0) | (chip == half - 1)

        def own_rest():
            send_second(me, 0, aside)
            send_first(me, 1, above)

        pl.when(outer)(own_rest)
        o_part(aside, 0, partner).wait_recv()
        o_part(aside, 2, above).start()

        @pl.when(aside < n - 1)
        def _():
            top_part(aside, 0, partner).wait_recv()
            top_part(aside, 2, above).start()

        used(above, lambda: bottom_part(above, 0, partner).wait_recv())
        send_second(above, 2, aside)
        pl.when(jnp.logical_not(outer))(own_rest)
    else:
        for k, target in enumerate(targets):
            send_first(me, k, target)
            send_second(me, k, target)

    def o_forward(j):
        return remote(o_buf.at[j], o_buf.at[j], o_fsend.at[j], o_recv.at[j], partner)

    def m_forward(j):
        return remote(m_buf.at[j], m_buf.at[j], m_fsend.at[j], m_recv.at[j], partner)

    def s_forward(t):
        return remote(hist.at[t], other.at[t], s_send.at[t], s_recv.at[t], partner)

    row_at = lax.broadcasted_iota(jnp.int32, (w, w), 0)
    column_at = lax.broadcasted_iota(jnp.int32, (w, w), 1)
    eye = row_at == column_at
    energy = energy_floor + energy_spacing * index_ref[mine].astype(f32)

    def scaled(real, imag):
        diag_real = jnp.sum(jnp.where(eye, real, 0.0), axis=0, keepdims=True)
        diag_imag = jnp.sum(jnp.where(eye, imag, 0.0), axis=0, keepdims=True)
        modulus = diag_real * diag_real + diag_imag * diag_imag
        xr = diag_real / modulus
        xi = -diag_imag / modulus
        xrc = jnp.sum(jnp.where(eye, xr, 0.0), axis=1, keepdims=True)
        xic = jnp.sum(jnp.where(eye, xi, 0.0), axis=1, keepdims=True)
        off_real = jnp.where(eye, 0.0, real)
        off_imag = jnp.where(eye, 0.0, imag)
        fr = off_real * xr - off_imag * xi
        fi = off_real * xi + off_imag * xr
        return (xr, xi, xrc, xic), (off_real, off_imag), (fr, fi)

    def completed(x, f, left, f2):
        third = complex_product(left, f2)
        hr = jnp.where(eye, 1.0, 0.0) - f[0] + f2[0] - third[0]
        hi = f2[1] - f[1] - third[1]
        xrc, xic = x[2], x[3]
        return xrc * hr - xic * hi, xrc * hi + xic * hr

    def diagonal(x, off, f, f2):
        xr, xi, xrc, xic = x
        zr = off[0] * xrc - off[1] * xic
        zi = off[0] * xic + off[1] * xrc
        wr = f[0] - f2[0]
        wi = f[1] - f2[1]
        dr = 1.0 + jnp.sum(zr * wr - zi * wi, axis=0, keepdims=True)
        di = jnp.sum(zr * wi + zi * wr, axis=0, keepdims=True)
        return -2.0 * (xr * di + xi * dr)

    def matrix(t, slot):
        own = unpacked(slab_at(t))
        real = jnp.where(eye, energy, 0.0) - own - hist[slot, 0]
        imag = jnp.where(eye, broadening, 0.0) - hist[slot, 1]
        return real, imag

    def chain(t, a, slot):
        m = m_buf[coupling_at(t)]
        high, low = split(m)
        factor[side, 0] = high
        factor[side, 1] = low
        high, low = split(m.T)
        factor[1 - side, 0] = high
        factor[1 - side, 1] = low
        x, off, f = scaled(*a)
        left = rounded(*f)
        f2 = complex_product(left, f)
        g = completed(x, f, left, f2)
        gs = split(jnp.concatenate(g, axis=0))
        u = product(gs, (factor[0, 0], factor[0, 1]))
        us = split(jnp.concatenate([u[:w], u[w:]], axis=1))
        s = product((factor[1, 0], factor[1, 1]), us)
        hist[slot, 0] = s[:, :w]
        hist[slot, 1] = s[:, w:]

    def final(t, a):
        partner_real = other[n - 1 - t, 0]
        partner_imag = other[n - 1 - t, 1]
        x, off, f = scaled(a[0] - partner_real, a[1] - partner_imag)
        left = rounded(*f)
        f2 = complex_product(left, f)
        rows[t - half] = jnp.broadcast_to(diagonal(x, off, f, f2), (8, w))
        return x, f, left, f2

    rates = jnp.where(side == 0, rates_ref[0:1, :], rates_ref[1:2, :])
    hist[0, 0] = jnp.zeros((w, w), f32)
    hist[0, 1] = jnp.where(eye, -0.5 * rates, 0.0)

    def first_half(t, carry):
        a = slab_at(t)
        at_hand = (a % 2) == side
        held = jnp.where(at_hand, a, n - 1 - a)

        @pl.when((held != me) & (held != aside))
        def _():
            arrived(o_buf, o_recv, held)

        o_forward(held).start()
        b = coupling_at(t)
        c = n - 2 - b

        @pl.when((t % 2) == side)
        def _():
            direct(c)
            m_forward(c).start()

            @pl.when(b != c)
            def _():
                direct(b)
                m_forward(b).start()

        @pl.when((t % 2) != side)
        def _():
            arrived(m_buf, m_recv, b)

        @pl.when(jnp.logical_not(at_hand))
        def _():
            arrived(o_buf, o_recv, a)

        s_forward(t).start()
        chain(t, matrix(t, t), t + 1)
        return carry

    lax.fori_loop(0, half, first_half, 0)

    def later_waits(t, coupled):
        a = slab_at(t)

        @pl.when((a % 2) != side)
        def _():
            arrived(o_buf, o_recv, a)

        if coupled:
            @pl.when((t % 2) != side)
            def _():
                arrived(m_buf, m_recv, coupling_at(t))

        s_forward(n - 1 - t).wait_recv()

    def row_copy(t):
        return remote(
            rows.at[t - half], rows_in.at[mine], r_send.at[t - half], r_recv.at[mine], slab_at(t)
        )

    def deliver(t):
        target = slab_at(t)

        @pl.when((target // group) == (me // group))
        def _():
            @pl.when(target == me)
            def _():
                rows_in[mine] = rows[t - half]

            @pl.when(target != me)
            def _():
                row_copy(t).start()

    def t_copy(k):
        return remote(
            crossing_own, crossing_in.at[mine], t_send.at[k - 1], t_recv.at[mine],
            base + (me - base + k) % group,
        )

    later_waits(half, half < n - 1)
    a = matrix(half, half)
    gamma_left = -2.0 * hist[half, 1]
    x, f, left, f2 = final(half, a)
    gr, gi = completed(x, f, left, f2)
    gamma_right = -2.0 * other[half - 1, 1]
    forward = product(split(gamma_left), split(jnp.concatenate([gr, gi], axis=1)))
    backward = product(split(jnp.concatenate([gr, gi], axis=0)), split(gamma_right))
    total = jnp.sum(forward[:, :w] * backward[:w] + forward[:, w:] * backward[w:])
    crossing_own[...] = jnp.full((8, 128), total, f32)
    chain(half, a, half)

    def last_half(t, carry):
        later_waits(t, True)
        deliver(t - 1)
        a = matrix(t, half)
        final(t, a)
        chain(t, a, half)
        return carry

    lax.fori_loop(half + 1, n - 1, last_half, 0)

    @pl.when(side == 0)
    def _():
        crossing_in[mine] = crossing_own[...]
        for k in range(1, group):
            t_copy(k).start()

    later_waits(n - 1, False)
    deliver(n - 2)
    final(n - 1, matrix(n - 1, half))
    deliver(n - 1)

    def row_wait(e):
        remote(rows.at[0], rows_in.at[e], r_send.at[0], r_recv.at[e], partner).wait_recv()

    sender_side = jnp.where(me < half, 1, 0)
    for e in range(ne):
        pl.when(base + 2 * e + sender_side != me)(functools.partial(row_wait, e))

    def t_wait(e):
        remote(crossing_own, crossing_in.at[e], t_send.at[0], t_recv.at[e], partner).wait_recv()

    for e in range(ne):
        pl.when(base + 2 * e != me)(functools.partial(t_wait, e))
    for e in range(ne):
        spectral_ref[0, e : e + 1, :] = rows_in[e, 0:1, :]
        crossing_ref[e] = crossing_in[e, 0, 0]

    def sent_first(j, k):
        o_part(j, k, partner).wait_send()
        used(j, lambda: top_part(j, k, partner).wait_send())

    def sent_second(j, k):
        used(j, lambda: bottom_part(j, k, partner).wait_send())

    for k in range(len(targets)):
        sent_first(me, k)
        sent_second(me, k)
    if square:
        sent_first(aside, 2)
        sent_second(above, 2)

    @pl.when(side == 0)
    def _():
        for k in range(1, group):
            t_copy(k).wait_send()

    def drain(t, carry):
        a = slab_at(t)
        o_forward(jnp.where((a % 2) == side, a, n - 1 - a)).wait_send()
        b = coupling_at(t)
        c = n - 2 - b

        @pl.when((t % 2) == side)
        def _():
            m_forward(c).wait_send()

            @pl.when(b != c)
            def _():
                m_forward(b).wait_send()

        s_forward(t).wait_send()
        target = slab_at(t + half)

        @pl.when(((target // group) == (me // group)) & (target != me))
        def _():
            row_copy(t + half).wait_send()

        return carry

    lax.fori_loop(0, half, drain, 0)


def solution(mesh):
    n = mesh.shape["slab"]

    def on_device(onsite, coupling, pattern, contact_rates, energy_index):
        w = onsite.shape[1]
        ne = energy_index.shape[0]
        half = n // 2
        dma = pltpu.SemaphoreType.DMA
        return pl.pallas_call(
            functools.partial(kernel, n, ne, w),
            out_shape=(
                jax.ShapeDtypeStruct((1, ne, w), f32),
                jax.ShapeDtypeStruct((ne,), f32),
            ),
            in_specs=[
                pl.BlockSpec(memory_space=pl.ANY),
                pl.BlockSpec(memory_space=pl.ANY),
                pl.BlockSpec(memory_space=pltpu.SMEM),
                pl.BlockSpec(memory_space=pltpu.VMEM),
                pl.BlockSpec(memory_space=pltpu.SMEM),
            ],
            out_specs=(
                pl.BlockSpec(memory_space=pltpu.VMEM),
                pl.BlockSpec(memory_space=pltpu.SMEM),
            ),
            scratch_shapes=[
                pltpu.VMEM((2, w, w), f32),
                pltpu.VMEM((n, w // 2 + 8, w), f32),
                pltpu.VMEM((n, w, w), f32),
                pltpu.VMEM((half + 1, 2, w, w), f32),
                pltpu.VMEM((half, 2, w, w), f32),
                pltpu.VMEM((2, 2, w, w), bf16),
                pltpu.VMEM((half, 8, w), f32),
                pltpu.VMEM((8, 128), f32),
                pltpu.VMEM((ne, 8, w), f32),
                pltpu.VMEM((ne, 8, 128), f32),
                dma((2,)), dma((half - 1,)), dma((half - 1,)), dma((half - 1,)), dma((n,)), dma((n,)), dma((n,)), dma((n,)), dma((n,)),
                dma((half,)), dma((half,)), dma((half,)), dma((ne,)), dma((2 * ne - 1,)), dma((ne,)),
            ],
            compiler_params=pltpu.CompilerParams(
                collective_id=0, has_side_effects=True, vmem_limit_bytes=60 * 2**20
            ),
        )(onsite, coupling, pattern, contact_rates, energy_index)

    return jax.shard_map(
        on_device,
        mesh=mesh,
        in_specs=(
            P("slab", None, None),
            P("slab", None, None),
            P("slab", None, None),
            P(),
            P("energy"),
        ),
        out_specs=(P("slab", "energy", None), P("energy")),
        check_vma=False,
    )
```

```python
import functools

import jax
import jax.numpy as jnp
from jax import lax
from jax.experimental import pallas as pl
from jax.experimental.pallas import tpu as pltpu
from jax.sharding import PartitionSpec as P

energy_floor = -0.2
energy_spacing = 0.0125
broadening = 0.3
MESH = pl.DeviceIdType.MESH
f32, bf16 = jnp.float32, jnp.bfloat16


def split(x):
    high = x.astype(bf16)
    return high, (x - high.astype(f32)).astype(bf16)


def product(left, right):
    return jnp.dot(
        jnp.concatenate([left[0], left[0], left[1]], axis=1),
        jnp.concatenate([right[0], right[1], right[0]], axis=0),
        preferred_element_type=f32,
    )


def rounded(real, imag):
    return jnp.concatenate([real.astype(bf16), imag.astype(bf16)], axis=1)


def doubled(real, imag):
    real, imag = real.astype(bf16), imag.astype(bf16)
    return jnp.concatenate(
        [jnp.concatenate([real, imag], axis=1), jnp.concatenate([-imag, real], axis=1)], axis=0
    )


def complex_product(left, right):
    both = jnp.dot(left, doubled(*right), preferred_element_type=f32)
    width = both.shape[1] // 2
    return both[:, :width], both[:, width:]


def exclusive(index, other, count):
    if count & (count - 1):
        return (index + other) % count
    total, bit = 0, 1
    while bit < count:
        total = total + (((index // bit) + (other // bit) % 2) % 2) * bit
        bit *= 2
    return total


def kernel(
    n, ne, w,
    onsite_in, coupling_in, pattern_ref, rates_ref, index_ref,
    spectral_ref, crossing_ref,
    raw, o_buf, m_buf, bare, hist, other, current, factor, rows, crossing_own, rows_in, crossing_in,
    local_sem, o_send, m_send, o_relay, m_relay, f_send, o_recv, m_recv,
    s_send, s_recv, r_send, r_recv, t_send, t_recv,
):
    half = n // 2
    group = 2 * ne
    me = lax.axis_index("slab")
    side = me % 2
    partner = me + 1 - 2 * side
    chip = me // 2
    mine = chip % ne
    base = (me // group) * group
    square = half == 4

    def slab_at(t):
        return t + side * (n - 1 - 2 * t)

    def coupling_at(t):
        return t + side * (n - 2 - 2 * t)

    def remote(src, dst, send, recv, target):
        return pltpu.make_async_remote_copy(
            src_ref=src, dst_ref=dst, send_sem=send, recv_sem=recv,
            device_id={"slab": target}, device_id_type=MESH,
        )

    own_o = pltpu.make_async_copy(onsite_in.at[0], raw.at[0], local_sem.at[0])
    own_m = pltpu.make_async_copy(coupling_in.at[0], raw.at[1], local_sem.at[1])
    own_o.start()
    own_m.start()

    barrier = pltpu.get_barrier_semaphore()
    for step in range(1, n):
        pl.semaphore_signal(
            barrier, inc=1, device_id={"slab": (me + step) % n}, device_id_type=MESH
        )

    h = w // 2
    tile_row = lax.broadcasted_iota(jnp.int32, (h, h), 0)
    tile_column = lax.broadcasted_iota(jnp.int32, (h, h), 1)

    def packed(block):
        last = block[h:, h:]
        o_buf[me, :h, :h] = jnp.where(tile_row >= tile_column, block[:h, :h], last)
        o_buf[me, :h, h:] = block[:h, h:]
        diag = jnp.sum(jnp.where(tile_row == tile_column, last, 0.0), axis=0, keepdims=True)
        o_buf[me, h:, :] = jnp.broadcast_to(jnp.concatenate([diag, diag], axis=1), (8, w))

    def unpacked(j):
        both = o_buf[j, :h, :h]
        corner = o_buf[j, :h, h:]
        turned = both.T
        first = jnp.where(tile_row >= tile_column, both, turned)
        last = jnp.where(tile_row < tile_column, both, turned)
        last = jnp.where(tile_row == tile_column, o_buf[j, h : h + 1, :h], last)
        return jnp.concatenate(
            [
                jnp.concatenate([first, corner], axis=1),
                jnp.concatenate([corner.T, last], axis=1),
            ],
            axis=0,
        )

    own_o.wait()
    own_m.wait()
    packed(raw[0])
    tiles = pattern_ref.shape[1]
    size = w // tiles
    lane_tile = lax.broadcasted_iota(jnp.int32, (1, w), 1) // size
    for p in range(tiles):
        kept = jnp.zeros((1, w), f32)
        for q in range(tiles):
            kept = jnp.where(lane_tile == q, pattern_ref[0, p, q].astype(f32), kept)
        m_buf[me, p * size : (p + 1) * size, :] = raw[1, p * size : (p + 1) * size, :] * kept
    pl.semaphore_wait(barrier, n - 1)

    o_rows = o_buf.shape[1]
    o_cut = (o_rows // 16 + 1) * 8
    o_part = (pl.ds(0, o_cut), pl.ds(o_cut, o_rows - o_cut))
    m_part = (pl.ds(0, h), pl.ds(h, w - h))
    user = jnp.where(me < half, 0, 1)
    o_step = jnp.where(me < half, me, n - 1 - me)
    m_step = jnp.where(me < half, me, n - 2 - me)
    spread = (1, 2) if square else tuple(range(1, half))

    def stage(step):
        if not square:
            return jnp.zeros_like(step)
        return jnp.zeros_like(step)

    def o_copy(j, p, send, target):
        view = o_buf.at[j, o_part[p]]
        return remote(view, view, send, o_recv.at[j, p], target)

    def m_copy(j, p, send, target):
        view = m_buf.at[j, m_part[p]]
        return remote(view, view, send, m_recv.at[j, p], target)

    def own_copies(copy, send, act):
        for order in (0, 1):
            for k in spread:
                p = order if k == 1 else 1 - order
                act(copy(me, p, send.at[k, p], exclusive(chip, k, half) * 2 + user))

    def partner_copies(copy, send, act):
        @pl.when(side != user)
        def _():
            for p in (0, 1):
                act(copy(me, p, send.at[0, p], partner))

    def start(c):
        c.start()

    def finish(c):
        c.wait_send()

    def own_stage(s):
        pl.when(stage(o_step) == s)(lambda: own_copies(o_copy, o_send, start))
        pl.when((stage(m_step) == s) & (me < n - 1))(lambda: own_copies(m_copy, m_send, start))

    own_stage(0)
    partner_copies(o_copy, o_send, start)
    pl.when(me < n - 1)(lambda: partner_copies(m_copy, m_send, start))

    def passes(j, p):
        return chip == exclusive(j // 2, p + 1, half)

    def o_relayed(t, p):
        j = slab_at(t)
        return o_copy(j, p, o_relay.at[t], exclusive(chip, 2 - p, half) * 2 + side)

    def m_relayed(t, p):
        j = coupling_at(t)
        return m_copy(j, p, m_relay.at[t], exclusive(chip, 2 - p, half) * 2 + side)

    def m_shared(t):
        return (side == 1) & (t == half - 1)

    def relay_o(t):
        if square:
            for p in (0, 1):

                @pl.when(passes(slab_at(t), p))
                def _():
                    o_copy(slab_at(t), p, o_relay.at[t], partner).wait_recv()
                    o_relayed(t, p).start()

    def rest_o(t):
        j = slab_at(t)
        for p in (0, 1):
            waits = j != me
            if square:
                waits = waits & jnp.logical_not(passes(j, p))
            pl.when(waits)(lambda p=p: o_copy(j, p, o_relay.at[t], partner).wait_recv())

    def relay_m(t):
        if square:
            for p in (0, 1):

                @pl.when(passes(coupling_at(t), p) & jnp.logical_not(m_shared(t)))
                def _():
                    m_copy(coupling_at(t), p, m_relay.at[t], partner).wait_recv()
                    m_relayed(t, p).start()

    def handed(p):
        return m_copy(half - 1, p, f_send.at[p], partner)

    hands = (side == 0) & (partner != half - 1)

    def rest_m(t):
        j = coupling_at(t)
        for p in (0, 1):
            waits = j != me
            if square:
                waits = waits & (jnp.logical_not(passes(j, p)) | m_shared(t))
            pl.when(waits)(lambda p=p: m_copy(j, p, m_relay.at[t], partner).wait_recv())

        @pl.when(hands & (t == half - 1))
        def _():
            for p in (0, 1):
                handed(p).start()

    row_at = lax.broadcasted_iota(jnp.int32, (w, w), 0)
    column_at = lax.broadcasted_iota(jnp.int32, (w, w), 1)
    eye = row_at == column_at
    energy = energy_floor + energy_spacing * index_ref[mine].astype(f32)

    def scaled(real, imag):
        diag_real = jnp.sum(jnp.where(eye, real, 0.0), axis=0, keepdims=True)
        diag_imag = jnp.sum(jnp.where(eye, imag, 0.0), axis=0, keepdims=True)
        modulus = diag_real * diag_real + diag_imag * diag_imag
        xr = diag_real / modulus
        xi = -diag_imag / modulus
        xrc = jnp.sum(jnp.where(eye, xr, 0.0), axis=1, keepdims=True)
        xic = jnp.sum(jnp.where(eye, xi, 0.0), axis=1, keepdims=True)
        off_real = jnp.where(eye, 0.0, real)
        off_imag = jnp.where(eye, 0.0, imag)
        fr = off_real * xr - off_imag * xi
        fi = off_real * xi + off_imag * xr
        return (xr, xi, xrc, xic), (off_real, off_imag), (fr, fi)

    def completed(x, f, left, f2):
        third = complex_product(left, f2)
        hr = jnp.where(eye, 1.0, 0.0) - f[0] + f2[0] - third[0]
        hi = f2[1] - f[1] - third[1]
        xrc, xic = x[2], x[3]
        return xrc * hr - xic * hi, xrc * hi + xic * hr

    def diagonal(x, off, f, f2):
        xr, xi, xrc, xic = x
        zr = off[0] * xrc - off[1] * xic
        zi = off[0] * xic + off[1] * xrc
        wr = f[0] - f2[0]
        wi = f[1] - f2[1]
        dr = 1.0 + jnp.sum(zr * wr - zi * wi, axis=0, keepdims=True)
        di = jnp.sum(zr * wi + zi * wr, axis=0, keepdims=True)
        return -2.0 * (xr * di + xi * dr)

    def keep_factor(t):
        m = m_buf[coupling_at(t)]
        high, low = split(m)
        factor[t, side, 0] = high
        factor[t, side, 1] = low
        high, low = split(m.T)
        factor[t, 1 - side, 0] = high
        factor[t, 1 - side, 1] = low

    def inverted(a):
        x, off, f = scaled(*a)
        left = rounded(*f)
        f2 = complex_product(left, f)
        return completed(x, f, left, f2)

    def stepped(g, first, second, out):
        gs = split(jnp.concatenate(g, axis=0))
        u = product(gs, (first[0], first[1]))
        us = split(jnp.concatenate([u[:w], u[w:]], axis=1))
        s = product((second[0], second[1]), us)
        out[0] = s[:, :w]
        out[1] = s[:, w:]

    def final(k, real, imag):
        x, off, f = scaled(real, imag)
        left = rounded(*f)
        f2 = complex_product(left, f)
        rows[k] = jnp.broadcast_to(diagonal(x, off, f, f2), (8, w))
        return x, f, left, f2

    rates = jnp.where(side == 0, rates_ref[0:1, :], rates_ref[1:2, :])
    hist[0, 0] = jnp.zeros((w, w), f32)
    hist[0, 1] = jnp.where(eye, -0.5 * rates, 0.0)
    widths = jnp.where(eye, broadening, 0.0)

    if square:
        for t in range(half):
            relay_o(t)
            relay_m(t)

    def outward(t, carry):
        rest_o(t)
        level = jnp.where(eye, energy, 0.0) - unpacked(slab_at(t))
        bare[t] = level
        g = inverted((level - hist[t, 0], widths - hist[t, 1]))
        rest_m(t)
        keep_factor(t)
        stepped(g, factor.at[t, 0], factor.at[t, 1], hist.at[t + 1])
        return carry

    lax.fori_loop(0, half, outward, 0)

    swap = remote(hist.at[half], other, s_send.at[0], s_recv.at[0], partner)
    swap.start()

    def row_copy(k):
        return remote(
            rows.at[k], rows_in.at[mine], r_send.at[k], r_recv.at[mine], slab_at(half - 1 - k)
        )

    def deliver(k):
        target = slab_at(half - 1 - k)

        @pl.when((target // group) == (me // group))
        def _():
            @pl.when(target == me)
            def _():
                rows_in[mine] = rows[k]

            @pl.when(target != me)
            def _():
                row_copy(k).start()

    def t_copy(k):
        return remote(
            crossing_own, crossing_in.at[mine], t_send.at[k - 1], t_recv.at[mine],
            base + (me - base + k) % group,
        )

    def behind(t, g):
        stepped(g, factor.at[t, 1], factor.at[t, 0], current)

    last = half - 1
    swap.wait_recv()
    real = bare[last] - other[0]
    imag = widths - other[1]
    x, f, left, f2 = final(0, real - hist[last, 0], imag - hist[last, 1])

    @pl.when(side == 1)
    def _():
        gr, gi = completed(x, f, left, f2)
        gamma_left = -2.0 * other[1]
        gamma_right = -2.0 * hist[last, 1]
        forward = product(split(gamma_left), split(jnp.concatenate([gr, gi], axis=1)))
        backward = product(split(jnp.concatenate([gr, gi], axis=0)), split(gamma_right))
        total = jnp.sum(forward[:, :w] * backward[:w] + forward[:, w:] * backward[w:])
        crossing_own[...] = jnp.full((8, 128), total, f32)

    behind(last - 1, inverted((real, imag)))

    def inward(k, carry):
        deliver(k - 1)
        t = last - k
        real = bare[t] - current[0]
        imag = widths - current[1]
        final(k, real - hist[t, 0], imag - hist[t, 1])
        behind(t - 1, inverted((real, imag)))
        return carry

    lax.fori_loop(1, last, inward, 0)

    @pl.when(side == 1)
    def _():
        crossing_in[mine] = crossing_own[...]
        for k in range(1, group):
            t_copy(k).start()

    deliver(last - 1)
    final(last, bare[0] - current[0] - hist[0, 0], widths - current[1] - hist[0, 1])
    deliver(last)

    def row_wait(e):
        remote(rows.at[0], rows_in.at[e], r_send.at[0], r_recv.at[e], partner).wait_recv()

    for e in range(ne):
        pl.when(base + 2 * e + user != me)(functools.partial(row_wait, e))

    def t_wait(e):
        remote(crossing_own, crossing_in.at[e], t_send.at[0], t_recv.at[e], partner).wait_recv()

    for e in range(ne):
        pl.when(base + 2 * e + 1 != me)(functools.partial(t_wait, e))
    for e in range(ne):
        spectral_ref[0, e : e + 1, :] = rows_in[e, 0:1, :]
        crossing_ref[e] = crossing_in[e, 0, 0]

    own_copies(o_copy, o_send, finish)
    partner_copies(o_copy, o_send, finish)

    @pl.when(me < n - 1)
    def _():
        own_copies(m_copy, m_send, finish)
        partner_copies(m_copy, m_send, finish)

    @pl.when(hands)
    def _():
        for p in (0, 1):
            handed(p).wait_send()

    swap.wait_send()

    @pl.when(side == 1)
    def _():
        for k in range(1, group):
            t_copy(k).wait_send()

    def drain(t, carry):
        if square:
            for p in (0, 1):
                pl.when(passes(slab_at(t), p))(lambda p=p: o_relayed(t, p).wait_send())
                pl.when(passes(coupling_at(t), p) & jnp.logical_not(m_shared(t)))(
                    lambda p=p: m_relayed(t, p).wait_send()
                )
        target = slab_at(half - 1 - t)

        @pl.when(((target // group) == (me // group)) & (target != me))
        def _():
            row_copy(t).wait_send()

        return carry

    lax.fori_loop(0, half, drain, 0)


def solution(mesh):
    n = mesh.shape["slab"]

    def on_device(onsite, coupling, pattern, contact_rates, energy_index):
        w = onsite.shape[1]
        ne = energy_index.shape[0]
        half = n // 2
        dma = pltpu.SemaphoreType.DMA
        return pl.pallas_call(
            functools.partial(kernel, n, ne, w),
            out_shape=(
                jax.ShapeDtypeStruct((1, ne, w), f32),
                jax.ShapeDtypeStruct((ne,), f32),
            ),
            in_specs=[
                pl.BlockSpec(memory_space=pl.ANY),
                pl.BlockSpec(memory_space=pl.ANY),
                pl.BlockSpec(memory_space=pltpu.SMEM),
                pl.BlockSpec(memory_space=pltpu.VMEM),
                pl.BlockSpec(memory_space=pltpu.SMEM),
            ],
            out_specs=(
                pl.BlockSpec(memory_space=pltpu.VMEM),
                pl.BlockSpec(memory_space=pltpu.SMEM),
            ),
            scratch_shapes=[
                pltpu.VMEM((2, w, w), f32),
                pltpu.VMEM((n, w // 2 + 8, w), f32),
                pltpu.VMEM((n, w, w), f32),
                pltpu.VMEM((half, w, w), f32),
                pltpu.VMEM((half + 1, 2, w, w), f32),
                pltpu.VMEM((2, w, w), f32),
                pltpu.VMEM((2, w, w), f32),
                pltpu.VMEM((half, 2, 2, w, w), bf16),
                pltpu.VMEM((half, 8, w), f32),
                pltpu.VMEM((8, 128), f32),
                pltpu.VMEM((ne, 8, w), f32),
                pltpu.VMEM((ne, 8, 128), f32),
                dma((2,)), dma((half, 2)), dma((half, 2)), dma((half,)), dma((half,)), dma((2,)), dma((n, 2)), dma((n, 2)),
                dma((1,)), dma((1,)), dma((half,)), dma((ne,)), dma((2 * ne - 1,)), dma((ne,)),
            ],
            compiler_params=pltpu.CompilerParams(
                collective_id=0, has_side_effects=True, vmem_limit_bytes=60 * 2**20
            ),
        )(onsite, coupling, pattern, contact_rates, energy_index)

    return jax.shard_map(
        on_device,
        mesh=mesh,
        in_specs=(
            P("slab", None, None),
            P("slab", None, None),
            P("slab", None, None),
            P(),
            P("energy"),
        ),
        out_specs=(P("slab", "energy", None), P("energy")),
        check_vma=False,
    )
```

```python
import functools

import jax
import jax.numpy as jnp
from jax import lax
from jax.experimental import pallas as pl
from jax.experimental.pallas import tpu as pltpu
from jax.sharding import PartitionSpec as P

energy_floor = -0.2
energy_spacing = 0.0125
broadening = 0.3
MESH = pl.DeviceIdType.MESH
f32, bf16 = jnp.float32, jnp.bfloat16


def split(x):
    high = x.astype(bf16)
    return high, (x - high.astype(f32)).astype(bf16)


def product(left, right):
    return jnp.dot(
        jnp.concatenate([left[0], left[0], left[1]], axis=1),
        jnp.concatenate([right[0], right[1], right[0]], axis=0),
        preferred_element_type=f32,
    )


def rounded(real, imag):
    return jnp.concatenate([real.astype(bf16), imag.astype(bf16)], axis=1)


def doubled(real, imag):
    real, imag = real.astype(bf16), imag.astype(bf16)
    return jnp.concatenate(
        [jnp.concatenate([real, imag], axis=1), jnp.concatenate([-imag, real], axis=1)], axis=0
    )


def complex_product(left, right):
    both = jnp.dot(left, doubled(*right), preferred_element_type=f32)
    width = both.shape[1] // 2
    return both[:, :width], both[:, width:]


def exclusive(index, other, count):
    if count & (count - 1):
        return (index + other) % count
    total, bit = 0, 1
    while bit < count:
        total = total + (((index // bit) + (other // bit) % 2) % 2) * bit
        bit *= 2
    return total


def kernel(
    n, ne, w,
    onsite_in, coupling_in, pattern_ref, rates_ref, index_ref,
    spectral_ref, crossing_ref,
    raw, o_buf, m_buf, bare, hist, other, current, factor, rows, crossing_own, rows_in, crossing_in,
    local_sem, o_send, m_send, o_relay, m_relay, f_send, o_recv, m_recv,
    s_send, s_recv, r_send, r_recv, t_send, t_recv,
):
    half = n // 2
    group = 2 * ne
    me = lax.axis_index("slab")
    side = me % 2
    partner = me + 1 - 2 * side
    chip = me // 2
    mine = chip % ne
    base = (me // group) * group
    square = half == 4

    def slab_at(t):
        return t + side * (n - 1 - 2 * t)

    def coupling_at(t):
        return t + side * (n - 2 - 2 * t)

    def remote(src, dst, send, recv, target):
        return pltpu.make_async_remote_copy(
            src_ref=src, dst_ref=dst, send_sem=send, recv_sem=recv,
            device_id={"slab": target}, device_id_type=MESH,
        )

    own_o = pltpu.make_async_copy(onsite_in.at[0], raw.at[0], local_sem.at[0])
    own_m = pltpu.make_async_copy(coupling_in.at[0], raw.at[1], local_sem.at[1])
    own_o.start()
    own_m.start()

    barrier = pltpu.get_barrier_semaphore()
    for step in range(1, n):
        pl.semaphore_signal(
            barrier, inc=1, device_id={"slab": (me + step) % n}, device_id_type=MESH
        )

    h = w // 2
    tile_row = lax.broadcasted_iota(jnp.int32, (h, h), 0)
    tile_column = lax.broadcasted_iota(jnp.int32, (h, h), 1)

    def packed(block):
        last = block[h:, h:]
        o_buf[me, :h, :h] = jnp.where(tile_row >= tile_column, block[:h, :h], last)
        o_buf[me, :h, h:] = block[:h, h:]
        diag = jnp.sum(jnp.where(tile_row == tile_column, last, 0.0), axis=0, keepdims=True)
        o_buf[me, h:, :] = jnp.broadcast_to(jnp.concatenate([diag, diag], axis=1), (8, w))

    def unpacked(j):
        both = o_buf[j, :h, :h]
        corner = o_buf[j, :h, h:]
        turned = both.T
        first = jnp.where(tile_row >= tile_column, both, turned)
        last = jnp.where(tile_row < tile_column, both, turned)
        last = jnp.where(tile_row == tile_column, o_buf[j, h : h + 1, :h], last)
        return jnp.concatenate(
            [
                jnp.concatenate([first, corner], axis=1),
                jnp.concatenate([corner.T, last], axis=1),
            ],
            axis=0,
        )

    own_o.wait()
    own_m.wait()
    packed(raw[0])
    tiles = pattern_ref.shape[1]
    size = w // tiles
    lane_tile = lax.broadcasted_iota(jnp.int32, (1, w), 1) // size
    for p in range(tiles):
        kept = jnp.zeros((1, w), f32)
        for q in range(tiles):
            kept = jnp.where(lane_tile == q, pattern_ref[0, p, q].astype(f32), kept)
        m_buf[me, p * size : (p + 1) * size, :] = raw[1, p * size : (p + 1) * size, :] * kept
    pl.semaphore_wait(barrier, n - 1)

    o_rows = o_buf.shape[1]
    o_cut = (o_rows // 16 + 1) * 8
    o_part = (pl.ds(0, o_cut), pl.ds(o_cut, o_rows - o_cut))
    m_part = (pl.ds(0, h), pl.ds(h, w - h))
    user = jnp.where(me < half, 0, 1)
    spread = (1, 2) if square else tuple(range(1, half))

    def o_copy(j, p, send, target):
        view = o_buf.at[j, o_part[p]]
        return remote(view, view, send, o_recv.at[j, p], target)

    def m_copy(j, p, send, target):
        view = m_buf.at[j, m_part[p]]
        return remote(view, view, send, m_recv.at[j, p], target)

    def own_copies(copy, send, act, orders=(0, 1)):
        for order in orders:
            for k in spread:
                p = order if k == 1 else 1 - order
                act(copy(me, p, send.at[k, p], exclusive(chip, k, half) * 2 + user))

    def partner_copies(copy, send, act):
        @pl.when(side != user)
        def _():
            for p in (0, 1):
                act(copy(me, p, send.at[0, p], partner))

    def start(c):
        c.start()

    def finish(c):
        c.wait_send()

    def send(order):
        own_copies(o_copy, o_send, start, (order,))
        pl.when(me < n - 1)(lambda: own_copies(m_copy, m_send, start, (order,)))

    passing = (chip != 0) & (chip != half - 1)
    send(0)
    if square:
        pl.when(jnp.logical_not(passing))(lambda: send(1))
    else:
        send(1)
    partner_copies(o_copy, o_send, start)
    pl.when(me < n - 1)(lambda: partner_copies(m_copy, m_send, start))

    def passes(j, p):
        return chip == exclusive(j // 2, p + 1, half)

    def o_relayed(t, p):
        j = slab_at(t)
        return o_copy(j, p, o_relay.at[t], exclusive(chip, 2 - p, half) * 2 + side)

    def m_relayed(t, p):
        j = coupling_at(t)
        return m_copy(j, p, m_relay.at[t], exclusive(chip, 2 - p, half) * 2 + side)

    def m_shared(t):
        return (side == 1) & (t == half - 1)

    def relay_o(t):
        if square:
            for p in (0, 1):

                @pl.when(passes(slab_at(t), p))
                def _():
                    o_copy(slab_at(t), p, o_relay.at[t], partner).wait_recv()
                    o_relayed(t, p).start()

    def rest_o(t):
        j = slab_at(t)
        for p in (0, 1):
            waits = j != me
            if square:
                waits = waits & jnp.logical_not(passes(j, p))
            pl.when(waits)(lambda p=p: o_copy(j, p, o_relay.at[t], partner).wait_recv())

    def relay_m(t):
        if square:
            for p in (0, 1):

                @pl.when(passes(coupling_at(t), p) & jnp.logical_not(m_shared(t)))
                def _():
                    m_copy(coupling_at(t), p, m_relay.at[t], partner).wait_recv()
                    m_relayed(t, p).start()

    def handed(p):
        return m_copy(half - 1, p, f_send.at[p], partner)

    hands = (side == 0) & (partner != half - 1)

    def rest_m(t):
        j = coupling_at(t)
        for p in (0, 1):
            waits = j != me
            if square:
                waits = waits & (jnp.logical_not(passes(j, p)) | m_shared(t))
            pl.when(waits)(lambda p=p: m_copy(j, p, m_relay.at[t], partner).wait_recv())

        @pl.when(hands & (t == half - 1))
        def _():
            for p in (0, 1):
                handed(p).start()

    row_at = lax.broadcasted_iota(jnp.int32, (w, w), 0)
    column_at = lax.broadcasted_iota(jnp.int32, (w, w), 1)
    eye = row_at == column_at
    energy = energy_floor + energy_spacing * index_ref[mine].astype(f32)

    def scaled(real, imag):
        diag_real = jnp.sum(jnp.where(eye, real, 0.0), axis=0, keepdims=True)
        diag_imag = jnp.sum(jnp.where(eye, imag, 0.0), axis=0, keepdims=True)
        modulus = diag_real * diag_real + diag_imag * diag_imag
        xr = diag_real / modulus
        xi = -diag_imag / modulus
        xrc = jnp.sum(jnp.where(eye, xr, 0.0), axis=1, keepdims=True)
        xic = jnp.sum(jnp.where(eye, xi, 0.0), axis=1, keepdims=True)
        off_real = jnp.where(eye, 0.0, real)
        off_imag = jnp.where(eye, 0.0, imag)
        fr = off_real * xr - off_imag * xi
        fi = off_real * xi + off_imag * xr
        return (xr, xi, xrc, xic), (off_real, off_imag), (fr, fi)

    def completed(x, f, left, f2):
        third = complex_product(left, f2)
        hr = jnp.where(eye, 1.0, 0.0) - f[0] + f2[0] - third[0]
        hi = f2[1] - f[1] - third[1]
        xrc, xic = x[2], x[3]
        return xrc * hr - xic * hi, xrc * hi + xic * hr

    def diagonal(x, off, f, f2):
        xr, xi, xrc, xic = x
        zr = off[0] * xrc - off[1] * xic
        zi = off[0] * xic + off[1] * xrc
        wr = f[0] - f2[0]
        wi = f[1] - f2[1]
        dr = 1.0 + jnp.sum(zr * wr - zi * wi, axis=0, keepdims=True)
        di = jnp.sum(zr * wi + zi * wr, axis=0, keepdims=True)
        return -2.0 * (xr * di + xi * dr)

    def keep_factor(t):
        m = m_buf[coupling_at(t)]
        high, low = split(m)
        factor[t, side, 0] = high
        factor[t, side, 1] = low
        high, low = split(m.T)
        factor[t, 1 - side, 0] = high
        factor[t, 1 - side, 1] = low

    def inverted(a):
        x, off, f = scaled(*a)
        left = rounded(*f)
        f2 = complex_product(left, f)
        return completed(x, f, left, f2)

    def stepped(g, first, second, out):
        gs = split(jnp.concatenate(g, axis=0))
        u = product(gs, (first[0], first[1]))
        us = split(jnp.concatenate([u[:w], u[w:]], axis=1))
        s = product((second[0], second[1]), us)
        out[0] = s[:, :w]
        out[1] = s[:, w:]

    def final(k, real, imag):
        x, off, f = scaled(real, imag)
        left = rounded(*f)
        f2 = complex_product(left, f)
        rows[k] = jnp.broadcast_to(diagonal(x, off, f, f2), (8, w))
        return x, f, left, f2

    rates = jnp.where(side == 0, rates_ref[0:1, :], rates_ref[1:2, :])
    hist[0, 0] = jnp.zeros((w, w), f32)
    hist[0, 1] = jnp.where(eye, -0.5 * rates, 0.0)
    widths = jnp.where(eye, broadening, 0.0)

    if square:
        for t in range(half):
            relay_o(t)
            relay_m(t)
        pl.when(passing)(lambda: send(1))

    def outward(t, carry):
        rest_o(t)
        level = jnp.where(eye, energy, 0.0) - unpacked(slab_at(t))
        bare[t] = level
        g = inverted((level - hist[t, 0], widths - hist[t, 1]))
        rest_m(t)
        keep_factor(t)
        stepped(g, factor.at[t, 0], factor.at[t, 1], hist.at[t + 1])
        return carry

    lax.fori_loop(0, half, outward, 0)

    swap = remote(hist.at[half], other, s_send.at[0], s_recv.at[0], partner)
    swap.start()

    def row_copy(k):
        return remote(
            rows.at[k], rows_in.at[mine], r_send.at[k], r_recv.at[mine], slab_at(half - 1 - k)
        )

    def deliver(k):
        target = slab_at(half - 1 - k)

        @pl.when((target // group) == (me // group))
        def _():
            @pl.when(target == me)
            def _():
                rows_in[mine] = rows[k]

            @pl.when(target != me)
            def _():
                row_copy(k).start()

    def t_copy(k):
        return remote(
            crossing_own, crossing_in.at[mine], t_send.at[k - 1], t_recv.at[mine],
            base + (me - base + k) % group,
        )

    def behind(t, g):
        stepped(g, factor.at[t, 1], factor.at[t, 0], current)

    last = half - 1
    swap.wait_recv()
    real = bare[last] - other[0]
    imag = widths - other[1]
    x, f, left, f2 = final(0, real - hist[last, 0], imag - hist[last, 1])

    @pl.when(side == 1)
    def _():
        gr, gi = completed(x, f, left, f2)
        gamma_left = -2.0 * other[1]
        gamma_right = -2.0 * hist[last, 1]
        forward = product(split(gamma_left), split(jnp.concatenate([gr, gi], axis=1)))
        backward = product(split(jnp.concatenate([gr, gi], axis=0)), split(gamma_right))
        total = jnp.sum(forward[:, :w] * backward[:w] + forward[:, w:] * backward[w:])
        crossing_own[...] = jnp.full((8, 128), total, f32)

    behind(last - 1, inverted((real, imag)))

    def inward(k, carry):
        deliver(k - 1)
        t = last - k
        real = bare[t] - current[0]
        imag = widths - current[1]
        final(k, real - hist[t, 0], imag - hist[t, 1])
        behind(t - 1, inverted((real, imag)))
        return carry

    lax.fori_loop(1, last, inward, 0)

    @pl.when(side == 1)
    def _():
        crossing_in[mine] = crossing_own[...]
        for k in range(1, group):
            t_copy(k).start()

    deliver(last - 1)
    final(last, bare[0] - current[0] - hist[0, 0], widths - current[1] - hist[0, 1])
    deliver(last)

    def row_wait(e):
        remote(rows.at[0], rows_in.at[e], r_send.at[0], r_recv.at[e], partner).wait_recv()

    for e in range(ne):
        pl.when(base + 2 * e + user != me)(functools.partial(row_wait, e))

    def t_wait(e):
        remote(crossing_own, crossing_in.at[e], t_send.at[0], t_recv.at[e], partner).wait_recv()

    for e in range(ne):
        pl.when(base + 2 * e + 1 != me)(functools.partial(t_wait, e))
    for e in range(ne):
        spectral_ref[0, e : e + 1, :] = rows_in[e, 0:1, :]
        crossing_ref[e] = crossing_in[e, 0, 0]

    own_copies(o_copy, o_send, finish)
    partner_copies(o_copy, o_send, finish)

    @pl.when(me < n - 1)
    def _():
        own_copies(m_copy, m_send, finish)
        partner_copies(m_copy, m_send, finish)

    @pl.when(hands)
    def _():
        for p in (0, 1):
            handed(p).wait_send()

    swap.wait_send()

    @pl.when(side == 1)
    def _():
        for k in range(1, group):
            t_copy(k).wait_send()

    def drain(t, carry):
        if square:
            for p in (0, 1):
                pl.when(passes(slab_at(t), p))(lambda p=p: o_relayed(t, p).wait_send())
                pl.when(passes(coupling_at(t), p) & jnp.logical_not(m_shared(t)))(
                    lambda p=p: m_relayed(t, p).wait_send()
                )
        target = slab_at(half - 1 - t)

        @pl.when(((target // group) == (me // group)) & (target != me))
        def _():
            row_copy(t).wait_send()

        return carry

    lax.fori_loop(0, half, drain, 0)


def solution(mesh):
    n = mesh.shape["slab"]

    def on_device(onsite, coupling, pattern, contact_rates, energy_index):
        w = onsite.shape[1]
        ne = energy_index.shape[0]
        half = n // 2
        dma = pltpu.SemaphoreType.DMA
        return pl.pallas_call(
            functools.partial(kernel, n, ne, w),
            out_shape=(
                jax.ShapeDtypeStruct((1, ne, w), f32),
                jax.ShapeDtypeStruct((ne,), f32),
            ),
            in_specs=[
                pl.BlockSpec(memory_space=pl.ANY),
                pl.BlockSpec(memory_space=pl.ANY),
                pl.BlockSpec(memory_space=pltpu.SMEM),
                pl.BlockSpec(memory_space=pltpu.VMEM),
                pl.BlockSpec(memory_space=pltpu.SMEM),
            ],
            out_specs=(
                pl.BlockSpec(memory_space=pltpu.VMEM),
                pl.BlockSpec(memory_space=pltpu.SMEM),
            ),
            scratch_shapes=[
                pltpu.VMEM((2, w, w), f32),
                pltpu.VMEM((n, w // 2 + 8, w), f32),
                pltpu.VMEM((n, w, w), f32),
                pltpu.VMEM((half, w, w), f32),
                pltpu.VMEM((half + 1, 2, w, w), f32),
                pltpu.VMEM((2, w, w), f32),
                pltpu.VMEM((2, w, w), f32),
                pltpu.VMEM((half, 2, 2, w, w), bf16),
                pltpu.VMEM((half, 8, w), f32),
                pltpu.VMEM((8, 128), f32),
                pltpu.VMEM((ne, 8, w), f32),
                pltpu.VMEM((ne, 8, 128), f32),
                dma((2,)), dma((half, 2)), dma((half, 2)), dma((half,)), dma((half,)), dma((2,)), dma((n, 2)), dma((n, 2)),
                dma((1,)), dma((1,)), dma((half,)), dma((ne,)), dma((2 * ne - 1,)), dma((ne,)),
            ],
            compiler_params=pltpu.CompilerParams(
                collective_id=0, has_side_effects=True, vmem_limit_bytes=60 * 2**20
            ),
        )(onsite, coupling, pattern, contact_rates, energy_index)

    return jax.shard_map(
        on_device,
        mesh=mesh,
        in_specs=(
            P("slab", None, None),
            P("slab", None, None),
            P("slab", None, None),
            P(),
            P("energy"),
        ),
        out_specs=(P("slab", "energy", None), P("energy")),
        check_vma=False,
    )
```
